32 devices in a mesh: groups: 2 (over y), ctx: 4 (over z), head: 2 (over x), sub: 2 (over core).
Axes of the slice: x: 2, y: 2, z: 4, core: 2. Of those that a mesh axis runs over, the one named last changes fastest.
Arguments:
- queries: bfloat16 [2048, 4096], P(('groups', 'ctx'), ('head', 'sub')), parts along dimension 0, may hold values from -24 to 24
- keys: bfloat16 [2048, 4096], P(('groups', 'ctx'), ('head', 'sub')), parts along dimension 0, may hold values from -24 to 24
- values: bfloat16 [2048, 4096], P(('groups', 'ctx'), ('head', 'sub')), parts along dimension 0, may hold values from -6 to 6
- mem_queries: bfloat16 [512, 4096], P('groups', ('head', 'sub')), parts along dimension 0, may hold values from -24 to 24
- mem_keys: bfloat16 [512, 4096], P('groups', ('head', 'sub')), parts along dimension 0, may hold values from -9 to 9
- mem_values: bfloat16 [512, 4096], P('groups', ('head', 'sub')), parts along dimension 0, may hold values from -6 to 6
- window_blocks: int32 [32, 5], P(('groups', 'ctx')), parts along dimension 0, may hold values from 0 to 15, as said below
- memory_blocks: int32 [32, 3], P(('groups', 'ctx')), parts along dimension 0, may hold values from 0 to 3, as said below
Outputs:
- attended: bfloat16 [2048, 4096], P(('groups', 'ctx'), ('head', 'sub')), parts along dimension 0
- memory_out: bfloat16 [512, 4096], P(('groups', 'ctx'), ('head', 'sub')), parts along dimension 0
The draws below stay inside these ranges and needn't reach their ends.
There are 2 independent parts, one for each index of `groups`. The reference program is written for one: setup_inputs(seed, part) draws one part's arguments, and reference() takes and returns one part's arrays. A program takes and returns all parts, laid end to end along the dimension named above; each array names one. Nothing has to cross between parts.
Inputs may be any that keep to these rules, and one draw needn't show every extreme that they name: `window_blocks`: entry [b, 0] is b itself; the 5 entries of row b are distinct blocks within 4 blocks of b. `memory_blocks`: each row holds 3 distinct memory blocks in increasing order.
All inputs are finite; a program needn't handle non-finite values.
Results may differ from the reference program's by a relative error of at most 0.004.
Values may be sent and summed in bfloat16 or wider, within the bound.
A program may use at most 128 MiB of HBM per device.

```python
import math
import jax
import jax.numpy as jnp
from jax import lax

HEADS = 32
HD = 128
MEM = 256
BLK = 64
RADIUS = 4
WSLOTS = 5
TOKENS = 1024
MSLOTS = 3


def joint_draw(key):
    columns = HEADS * HD
    base = jax.random.fold_in(key, 7)
    subkeys = jax.random.split(base, 4)
    queries = jax.random.normal(subkeys[0], (TOKENS, columns), jnp.float32)
    keyed = jax.random.normal(subkeys[2], (TOKENS, columns), jnp.float32)
    memory = 3.0 * jax.random.normal(subkeys[3], (MEM, columns), jnp.float32)
    return (jnp.clip(queries, -24.0, 24.0), jnp.clip(keyed, -24.0, 24.0), jnp.clip(memory, -24.0, 24.0))


def draw_queries(key, part):
    return joint_draw(key)[0].astype(jnp.bfloat16)


def draw_keys(key, part):
    return joint_draw(key)[1].astype(jnp.bfloat16)


def draw_mem_queries(key, part):
    return joint_draw(key)[2].astype(jnp.bfloat16)


def draw_window_blocks(key, part):
    block_count = TOKENS // BLK
    spread = 2 * RADIUS + 1
    blocks = jnp.arange(block_count)[:, None]
    offsets = jnp.arange(spread)[None, :] - RADIUS
    candidate = blocks + offsets
    inside = (candidate >= 0) & (candidate < block_count)
    noise = jax.random.randint(jax.random.fold_in(key, 3), (block_count, spread), 0, 1 << 20)
    ranking = noise * 16 + jnp.arange(spread)[None, :]
    ranking = jnp.where(offsets == 0, -1, jnp.where(inside, ranking, 1 << 28))
    ordering = jnp.argsort(ranking, axis=1)
    return jnp.take_along_axis(candidate, ordering[:, :WSLOTS], axis=1).astype(jnp.int32)


def draw_memory_blocks(key, part):
    block_count = TOKENS // BLK
    memory_count = MEM // BLK
    dropped = jax.random.randint(jax.random.fold_in(key, 5), (block_count, 1), 0, memory_count)
    row_index = jnp.arange(block_count)[:, None]
    dropped = jnp.where(row_index == 0, memory_count - 1, jnp.where(row_index == 1, 0, dropped))
    slots = jnp.arange(memory_count - 1)[None, :]
    return (slots + (slots >= dropped).astype(jnp.int32)).astype(jnp.int32)


def block_levels(own_key, shape, cuts, low, largest):
    factor_of, own = 1.0, jax.random.fold_in(own_key, 6)
    for dim, shards_of in cuts:
        draws = jnp.exp(jax.random.uniform(jax.random.fold_in(own, dim), (shards_of,), jnp.float32, low / len(cuts), largest / len(cuts)))
        factor_of = factor_of * jnp.repeat(draws, shape[dim] // shards_of).reshape([-1 if axis == dim else 1 for axis in range(len(shape))])
    return factor_of


def centred(rng, dims, deviation, most, shards=(), kind=jnp.bfloat16):
    values = deviation * jax.random.normal(rng, dims, jnp.float32)
    if shards:
        values = values * block_levels(rng, dims, shards, -0.22, 0.18)
    return jnp.clip(values, -most, most).astype(kind)


def setup_inputs(seed: int = 0, part: int = 0) -> dict:
    key_list = jax.random.split(jax.random.key(seed), 9)
    part_keys = jax.random.split(jax.random.fold_in(key_list[8], part), 9)
    return {
        "queries": draw_queries(jax.random.fold_in(jax.random.fold_in(key_list[8], part), 71), part),
        "keys": draw_keys(jax.random.fold_in(jax.random.fold_in(key_list[8], part), 71), part),
        "values": centred(part_keys[2], (TOKENS, HEADS * HD), 1.0, 6.0, ((0, 4), (1, 4))),
        "mem_queries": draw_mem_queries(jax.random.fold_in(jax.random.fold_in(key_list[8], part), 71), part),
        "mem_keys": centred(part_keys[4], (MEM, HEADS * HD), 1.5, 9.0, ((1, 4),)),
        "mem_values": centred(part_keys[5], (MEM, HEADS * HD), 1.0, 6.0, ((1, 4),)),
        "window_blocks": draw_window_blocks(jax.random.fold_in(jax.random.fold_in(key_list[8], part), 71), part),
        "memory_blocks": draw_memory_blocks(jax.random.fold_in(jax.random.fold_in(key_list[8], part), 71), part),
    }


def heads_first(array, row_count):
    return array.reshape(row_count, HEADS, HD).transpose(1, 0, 2)

def reference(queries, keys, values, mem_queries, mem_keys, mem_values, window_blocks, memory_blocks):
    block_count = TOKENS // BLK
    score_scale = 1.0 / math.sqrt(HD)
    slot_rows = (WSLOTS + MSLOTS) * BLK

    def token_head(item):
        query_head, key_head, value_head, memkey_head, memvalue_head = item
        key_rows = key_head.reshape(block_count, BLK, HD)
        value_rows = value_head.reshape(block_count, BLK, HD)
        memkey_rows = memkey_head.reshape(MEM // BLK, BLK, HD)
        memvalue_rows = memvalue_head.reshape(MEM // BLK, BLK, HD)
        key_set = jnp.concatenate([key_rows[window_blocks], memkey_rows[memory_blocks]], axis=1).reshape(block_count, slot_rows, HD)
        value_set = jnp.concatenate([value_rows[window_blocks], memvalue_rows[memory_blocks]], axis=1).reshape(block_count, slot_rows, HD)
        query_rows = query_head.reshape(block_count, BLK, HD)
        scores = jnp.einsum('nqd,nkd->nqk', query_rows.astype(jnp.float32), key_set.astype(jnp.float32)) * score_scale
        highest = lax.optimization_barrier(jnp.max(scores, axis=2, keepdims=True))
        exps = jnp.exp(scores - highest)
        totals = lax.optimization_barrier(jnp.sum(exps, axis=2, keepdims=True))
        weights = lax.optimization_barrier(exps.astype(jnp.bfloat16))
        summed = jnp.einsum('nqk,nkd->nqd', weights.astype(jnp.float32), value_set.astype(jnp.float32))
        return (summed / totals).reshape(TOKENS, HD).astype(jnp.bfloat16)

    def memory_head(item):
        memquery_head, key_head, value_head, memkey_head, memvalue_head = item
        all_keys = jnp.concatenate([key_head, memkey_head], axis=0).astype(jnp.float32)
        all_values = jnp.concatenate([value_head, memvalue_head], axis=0).astype(jnp.float32)
        scores = jnp.einsum('md,kd->mk', memquery_head.astype(jnp.float32), all_keys) * score_scale
        highest = lax.optimization_barrier(jnp.max(scores, axis=1, keepdims=True))
        exps = jnp.exp(scores - highest)
        totals = lax.optimization_barrier(jnp.sum(exps, axis=1, keepdims=True))
        weights = lax.optimization_barrier(exps.astype(jnp.bfloat16))
        summed = jnp.einsum('mk,kd->md', weights.astype(jnp.float32), all_values)
        return (summed / totals).astype(jnp.bfloat16)
    key_head_stack = heads_first(keys, TOKENS)
    value_heads = heads_first(values, TOKENS)
    memory_key_heads = heads_first(mem_keys, MEM)
    memvalue_heads = heads_first(mem_values, MEM)
    attended = lax.map(token_head, (heads_first(queries, TOKENS), key_head_stack, value_heads, memory_key_heads, memvalue_heads))
    memory_out = lax.map(memory_head, (heads_first(mem_queries, MEM), key_head_stack, value_heads, memory_key_heads, memvalue_heads))
    attended = attended.transpose(1, 0, 2).reshape(TOKENS, HEADS * HD)
    memory_out = memory_out.transpose(1, 0, 2).reshape(MEM, HEADS * HD)
    return (attended, memory_out)
```

```python
import functools
import math

import jax
import jax.numpy as jnp
from jax import lax
from jax.experimental import pallas as pl
from jax.experimental.pallas import tpu as pltpu
from jax.sharding import PartitionSpec as P

HD = 128
BLK = 64
RADIUS = 4
CHUNK_HEADS = 2
MESH = pl.DeviceIdType.MESH
EXPONENT_SCALE = math.log2(math.e) / math.sqrt(HD)
LOWEST = -1e30


def dot_nt(a, b):
    return lax.dot_general(a, b, (((1,), (1,)), ((), ())), preferred_element_type=jnp.float32)


def dot_nn(a, b):
    return lax.dot_general(a, b, (((1,), (0,)), ((), ())), preferred_element_type=jnp.float32)


def softmax_parts(scores):
    peak = jnp.max(scores, axis=1, keepdims=True)
    exps = jnp.exp2((scores - peak) * EXPONENT_SCALE)
    total = jnp.sum(exps, axis=1, keepdims=True)
    return peak, total, exps.astype(jnp.bfloat16)


def kernel(n, heads, rows, mem, chunks, *refs):
    (wb, mb, q_h, k_h, v_h, mq_h, mk_h, mv_h, out_h, mout_h) = refs[:10]
    refs = refs[10:]
    ext_k, ext_v, refs = refs[:chunks], refs[chunks : 2 * chunks], refs[2 * chunks :]
    (q_s, mq_s, mqo_s, mk_s, mv_s, out_s, mout_s, own_sum, own_stat, msg, msg_stat, got, got_stat) = refs[:13]
    (local_sem, kv_local, kv_send, kv_recv, p_send, p_recv, ps_send, ps_recv, out_sem) = refs[13:]

    per = heads // chunks
    width = per * HD
    own = mem // n
    blocks = rows // BLK
    halo = RADIUS * BLK
    me = lax.axis_index("ctx")
    has_low, has_high = me > 0, me < n - 1

    locals_ = [
        pltpu.make_async_copy(mq_h, mq_s, local_sem.at[0]),
        pltpu.make_async_copy(q_h, q_s, local_sem.at[1]),
        pltpu.make_async_copy(mk_h, mk_s, local_sem.at[2]),
        pltpu.make_async_copy(mv_h, mv_s, local_sem.at[3]),
        pltpu.make_async_copy(mq_h.at[pl.ds(pl.multiple_of(me * own, own), own)], mqo_s, local_sem.at[4]),
    ]
    kv_locals = []
    for c in range(chunks):
        cols = pl.ds(c * width, width)
        for t, (src, ext) in enumerate(((k_h, ext_k), (v_h, ext_v))):
            kv_locals.append(
                pltpu.make_async_copy(
                    src.at[:, :, cols], ext[c].at[pl.ds(RADIUS, blocks)], kv_local.at[c, t]
                )
            )
    locals_[0].start()
    for copy in kv_locals:
        copy.start()
    for copy in locals_[1:]:
        copy.start()

    barrier = pltpu.get_barrier_semaphore()
    for j in range(n):

        @pl.when(j != me)
        def _(j=j):
            pl.semaphore_signal(barrier, inc=1, device_id={"ctx": j}, device_id_type=MESH)

    pl.semaphore_wait(barrier, n - 1)

    high, low = jnp.minimum(me + 1, n - 1), jnp.maximum(me - 1, 0)

    def halo_copy(c, t, upward):
        src, ext = ((k_h, ext_k), (v_h, ext_v))[t]
        cols = pl.ds(c * width, width)
        d = 0 if upward else 1
        if upward:
            part, start, target = pl.ds(blocks - RADIUS, RADIUS), 0, high
        else:
            part, start, target = pl.ds(0, RADIUS), RADIUS + blocks, low
        return pltpu.make_async_remote_copy(
            src_ref=src.at[part, :, cols],
            dst_ref=ext[c].at[pl.ds(start, RADIUS)],
            send_sem=kv_send.at[c, t, d],
            recv_sem=kv_recv.at[c, t, d],
            device_id={"ctx": target},
            device_id_type=MESH,
        )

    def send_halo(c):
        @pl.when(has_high)
        def _():
            for t in range(2):
                halo_copy(c, t, True).start()

        @pl.when(has_low)
        def _():
            for t in range(2):
                halo_copy(c, t, False).start()

    early = (chunks + 1) // 2
    for c in range(early):
        send_halo(c)

    @pl.when(jnp.logical_not(has_low))
    def _():
        for c in range(chunks):
            ext_k[c][0:RADIUS] = jnp.zeros((RADIUS, BLK, width), jnp.bfloat16)
            ext_v[c][0:RADIUS] = jnp.zeros((RADIUS, BLK, width), jnp.bfloat16)

    @pl.when(jnp.logical_not(has_high))
    def _():
        for c in range(chunks):
            ext_k[c][RADIUS + blocks :] = jnp.zeros((RADIUS, BLK, width), jnp.bfloat16)
            ext_v[c][RADIUS + blocks :] = jnp.zeros((RADIUS, BLK, width), jnp.bfloat16)

    locals_[0].wait()
    lane = lax.broadcasted_iota(jnp.int32, (mem, HD), 1)
    stats = jnp.zeros((mem, HD), jnp.float32)
    for h in range(heads):
        c, o = h // per, (h % per) * HD
        if o == 0:
            kv_locals[2 * c].wait()
            kv_locals[2 * c + 1].wait()
        key = ext_k[c][RADIUS : RADIUS + blocks, :, o : o + HD].reshape(rows, HD)
        value = ext_v[c][RADIUS : RADIUS + blocks, :, o : o + HD].reshape(rows, HD)
        peak, total, weights = softmax_parts(dot_nt(mq_s[:, h * HD : (h + 1) * HD], key))
        part = dot_nn(weights, value) / total
        stats = jnp.where(lane == h, peak, stats)
        stats = jnp.where(lane == heads + h, total, stats)
        msg[:, :, h * HD : (h + 1) * HD] = part.reshape(n, own, HD).astype(jnp.bfloat16)
    stats = stats.reshape(n, own, HD)
    for j in range(n):
        msg_stat[j] = stats[j].T[: 2 * heads]

    def far(j):
        return jnp.logical_or(j - me >= 2, me - j >= 2)

    def partial_copies(slot, source, target):
        return (
            pltpu.make_async_remote_copy(
                src_ref=msg.at[slot],
                dst_ref=got.at[source],
                send_sem=p_send.at[slot],
                recv_sem=p_recv.at[source],
                device_id={"ctx": target},
                device_id_type=MESH,
            ),
            pltpu.make_async_remote_copy(
                src_ref=msg_stat.at[slot],
                dst_ref=got_stat.at[source],
                send_sem=ps_send.at[slot],
                recv_sem=ps_recv.at[source],
                device_id={"ctx": target},
                device_id_type=MESH,
            ),
        )

    for j in range(n):

        @pl.when(far(j))
        def _(j=j):
            for copy in partial_copies(j, me, j):
                copy.start()

    for c in range(early, chunks):
        send_halo(c)

    for copy in locals_[1:]:
        copy.wait()

    column = lax.broadcasted_iota(jnp.int32, (1, 2 * halo + rows + mem), 1)
    first = jnp.where(has_low, 0, halo)
    last = jnp.where(has_high, 2 * halo + rows, halo + rows)
    present = jnp.logical_or(
        jnp.logical_and(column >= first, column < last), column >= 2 * halo + rows
    )
    base = me * blocks - RADIUS

    def finish_memory(h):
        cols = slice(h * HD, (h + 1) * HD)
        mout_s[:, cols] = (own_sum[:, cols] / own_stat[:, heads + h : heads + h + 1]).astype(jnp.bfloat16)

    def fold(i, h):
        cols = slice(h * HD, (h + 1) * HD)
        columns = got_stat[i].T
        peak, total = own_stat[:, h : h + 1], own_stat[:, heads + h : heads + h + 1]
        other_peak, other_total = columns[:, h : h + 1], columns[:, heads + h : heads + h + 1]
        joined = jnp.maximum(peak, other_peak)
        factor = jnp.exp2((peak - joined) * EXPONENT_SCALE)
        other = other_total * jnp.exp2((other_peak - joined) * EXPONENT_SCALE)
        own_sum[:, cols] = own_sum[:, cols] * factor + got[i, :, cols].astype(jnp.float32) * other
        own_stat[:, h : h + 1] = joined
        own_stat[:, heads + h : heads + h + 1] = total * factor + other

    def fold_heads(some):
        for i in range(n):

            @pl.when(far(i))
            def _(i=i):
                for h in some:
                    fold(i, h)

        for h in some:
            finish_memory(h)

    for c in range(chunks):
        if c == chunks - 1:
            for i in range(n):

                @pl.when(far(i))
                def _(i=i):
                    for copy in partial_copies(i, i, i):
                        copy.wait_recv()

            fold_heads(range((chunks - 1) * per))

        @pl.when(has_low)
        def _(c=c):
            for t in range(2):
                halo_copy(c, t, True).wait_recv()

        @pl.when(has_high)
        def _(c=c):
            for t in range(2):
                halo_copy(c, t, False).wait_recv()

        for p in range(per):
            h, o = c * per + p, p * HD
            cols = slice(h * HD, (h + 1) * HD)
            for b in range(blocks):
                near = [
                    jnp.clip(wb[b, s] - base, 0, blocks + 2 * RADIUS - 1) for s in range(wb.shape[1])
                ]
                distant = [jnp.clip(mb[b, s], 0, mem // BLK - 1) for s in range(mb.shape[1])]
                key = jnp.concatenate(
                    [ext_k[c][s, :, o : o + HD] for s in near]
                    + [mk_s[s, :, cols] for s in distant],
                    axis=0,
                )
                value = jnp.concatenate(
                    [ext_v[c][s, :, o : o + HD] for s in near]
                    + [mv_s[s, :, cols] for s in distant],
                    axis=0,
                )
                part = slice(b * BLK, (b + 1) * BLK)
                peak, total, weights = softmax_parts(dot_nt(q_s[part, cols], key))
                out_s[part, cols] = (dot_nn(weights, value) / total).astype(jnp.bfloat16)
            query = mqo_s[:, cols]
            key = jnp.concatenate(
                [
                    ext_k[c][:, :, o : o + HD].reshape(rows + 2 * halo, HD),
                    mk_s[:, :, cols].reshape(mem, HD),
                ],
                axis=0,
            )
            value = jnp.concatenate(
                [
                    ext_v[c][:, :, o : o + HD].reshape(rows + 2 * halo, HD),
                    mv_s[:, :, cols].reshape(mem, HD),
                ],
                axis=0,
            )
            scores = jnp.where(present, dot_nt(query, key), LOWEST)
            peak, total, weights = softmax_parts(scores)
            own_sum[:, cols] = dot_nn(weights, value)
            own_stat[:, h : h + 1] = peak
            own_stat[:, heads + h : heads + h + 1] = total
        chunk_cols = pl.ds(c * width, width)
        pltpu.make_async_copy(out_s.at[:, chunk_cols], out_h.at[:, chunk_cols], out_sem.at[c]).start()

    fold_heads(range((chunks - 1) * per, heads))
    mem_out = pltpu.make_async_copy(mout_s, mout_h, out_sem.at[chunks])
    mem_out.start()

    for c in range(chunks):

        @pl.when(has_high)
        def _(c=c):
            for t in range(2):
                halo_copy(c, t, True).wait_send()

        @pl.when(has_low)
        def _(c=c):
            for t in range(2):
                halo_copy(c, t, False).wait_send()

    for j in range(n):

        @pl.when(far(j))
        def _(j=j):
            for copy in partial_copies(j, me, j):
                copy.wait_send()

    for c in range(chunks):
        chunk_cols = pl.ds(c * width, width)
        pltpu.make_async_copy(out_s.at[:, chunk_cols], out_h.at[:, chunk_cols], out_sem.at[c]).wait()
    mem_out.wait()


def on_device(
    n, queries, keys, values, mem_queries, mem_keys, mem_values, window_blocks, memory_blocks
):
    rows, columns = queries.shape
    mem = mem_queries.shape[0]
    heads = columns // HD
    chunks = heads // CHUNK_HEADS
    width = CHUNK_HEADS * HD
    own = mem // n
    ext_blocks = rows // BLK + 2 * RADIUS
    bf16, f32 = jnp.bfloat16, jnp.float32
    any_spec = pl.BlockSpec(memory_space=pl.ANY)
    smem_spec = pl.BlockSpec(memory_space=pltpu.SMEM)
    dma = pltpu.SemaphoreType.DMA
    scratch = (
        [pltpu.VMEM((ext_blocks, BLK, width), bf16) for _ in range(2 * chunks)]
        + [
            pltpu.VMEM((rows, columns), bf16),
            pltpu.VMEM((mem, columns), bf16),
            pltpu.VMEM((own, columns), bf16),
            pltpu.VMEM((mem // BLK, BLK, columns), bf16),
            pltpu.VMEM((mem // BLK, BLK, columns), bf16),
            pltpu.VMEM((rows, columns), bf16),
            pltpu.VMEM((own, columns), bf16),
            pltpu.VMEM((own, columns), f32),
            pltpu.VMEM((own, HD), f32),
            pltpu.VMEM((n, own, columns), bf16),
            pltpu.VMEM((n, 2 * heads, own), f32),
            pltpu.VMEM((n, own, columns), bf16),
            pltpu.VMEM((n, 2 * heads, own), f32),
        ]
        + [
            dma((5,)),
            dma((chunks, 2)),
            dma((chunks, 2, 2)),
            dma((chunks, 2, 2)),
            dma((n,)),
            dma((n,)),
            dma((n,)),
            dma((n,)),
            dma((chunks + 1,)),
        ]
    )

    def in_blocks(array):
        return array.reshape(-1, BLK, columns)

    return pl.pallas_call(
        functools.partial(kernel, n, heads, rows, mem, chunks),
        out_shape=(
            jax.ShapeDtypeStruct((rows, columns), bf16),
            jax.ShapeDtypeStruct((own, columns), bf16),
        ),
        in_specs=[smem_spec] * 2 + [any_spec] * 6,
        out_specs=(any_spec, any_spec),
        scratch_shapes=scratch,
        compiler_params=pltpu.CompilerParams(
            collective_id=0, has_side_effects=True, vmem_limit_bytes=60 << 20
        ),
        name="split_context_attention",
    )(
        window_blocks,
        memory_blocks,
        queries,
        in_blocks(keys),
        in_blocks(values),
        mem_queries,
        in_blocks(mem_keys),
        in_blocks(mem_values),
    )


def solution(mesh):
    in_specs = (
        P(("groups", "ctx"), ("head", "sub")),
        P(("groups", "ctx"), ("head", "sub")),
        P(("groups", "ctx"), ("head", "sub")),
        P("groups", ("head", "sub")),
        P("groups", ("head", "sub")),
        P("groups", ("head", "sub")),
        P(("groups", "ctx"), None),
        P(("groups", "ctx"), None),
    )
    out_specs = (P(("groups", "ctx"), ("head", "sub")), P(("groups", "ctx"), ("head", "sub")))
    return jax.shard_map(
        functools.partial(on_device, mesh.shape["ctx"]),
        mesh=mesh,
        in_specs=in_specs,
        out_specs=out_specs,
        check_vma=False,
    )
```

```python
import functools
import math

import jax
import jax.numpy as jnp
from jax import lax
from jax.experimental import pallas as pl
from jax.experimental.pallas import tpu as pltpu
from jax.sharding import PartitionSpec as P

HD = 128
BLK = 64
RADIUS = 4
MESH = pl.DeviceIdType.MESH
EXPONENT_SCALE = math.log2(math.e) / math.sqrt(HD)
LOWEST = -1e30
AHEAD = 3
PIECES = 4


def dot_nt(a, b):
    return lax.dot_general(a, b, (((1,), (1,)), ((), ())), preferred_element_type=jnp.float32)


def dot_nn(a, b):
    return lax.dot_general(a, b, (((1,), (0,)), ((), ())), preferred_element_type=jnp.float32)


def softmax_parts(scores):
    peak = jnp.max(scores, axis=1, keepdims=True)
    exps = jnp.exp2((scores - peak) * EXPONENT_SCALE)
    total = jnp.sum(exps, axis=1, keepdims=True)
    return peak, total, exps.astype(jnp.bfloat16)


def kernel(n, heads, rows, mem, groups, *refs):
    chunks = len(groups)
    (wb, mb, q_h, k_h, v_h, mq_h, mk_h, mv_h, out_h, mout_h) = refs[:10]
    refs = refs[10:]
    ext_k, ext_v, refs = refs[:chunks], refs[chunks : 2 * chunks], refs[2 * chunks :]
    (q_s, mq_s, mk_s, mv_s, out_s, mout_s, own_sum, own_stat, msg, msg_stat, got, got_stat) = refs[:12]
    (local_sem, kv_local, kv_send, kv_recv, p_send, p_recv, ps_send, ps_recv, out_sem) = refs[12:]

    def chunk_cols(c):
        return pl.ds(groups[c][0] * HD, groups[c][1] * HD)

    own = mem // n
    blocks = rows // BLK
    halo = RADIUS * BLK
    me = lax.axis_index("ctx")
    others = range(n // 2 - 1)
    has_low, has_high = me > 0, me < n - 1

    locals_ = [
        pltpu.make_async_copy(mq_h, mq_s, local_sem.at[0]),
        pltpu.make_async_copy(q_h, q_s, local_sem.at[1]),
        pltpu.make_async_copy(mk_h, mk_s, local_sem.at[2]),
        pltpu.make_async_copy(mv_h, mv_s, local_sem.at[3]),
    ]
    kv_locals = []
    for c in range(chunks):
        cols = chunk_cols(c)
        for t, (src, ext) in enumerate(((k_h, ext_k), (v_h, ext_v))):
            kv_locals.append(
                pltpu.make_async_copy(
                    src.at[:, :, cols], ext[c].at[pl.ds(RADIUS, blocks)], kv_local.at[c, t]
                )
            )
    locals_[0].start()
    for copy in kv_locals:
        copy.start()
    for copy in locals_[1:]:
        copy.start()

    barrier = pltpu.get_barrier_semaphore()
    for j in range(n):

        @pl.when(j != me)
        def _(j=j):
            pl.semaphore_signal(barrier, inc=1, device_id={"ctx": j}, device_id_type=MESH)

    pl.semaphore_wait(barrier, n - 1)

    high, low = jnp.minimum(me + 1, n - 1), jnp.maximum(me - 1, 0)

    def halo_copy(c, t, upward):
        src, ext = ((k_h, ext_k), (v_h, ext_v))[t]
        cols = chunk_cols(c)
        d = 0 if upward else 1
        if upward:
            part, start, target = pl.ds(blocks - RADIUS, RADIUS), 0, high
        else:
            part, start, target = pl.ds(0, RADIUS), RADIUS + blocks, low
        return pltpu.make_async_remote_copy(
            src_ref=src.at[part, :, cols],
            dst_ref=ext[c].at[pl.ds(start, RADIUS)],
            send_sem=kv_send.at[c, t, d],
            recv_sem=kv_recv.at[c, t, d],
            device_id={"ctx": target},
            device_id_type=MESH,
        )

    def send_halo(c):
        @pl.when(has_high)
        def _():
            for t in range(2):
                halo_copy(c, t, True).start()

        @pl.when(has_low)
        def _():
            for t in range(2):
                halo_copy(c, t, False).start()

    for c in range(min(AHEAD, chunks)):
        send_halo(c)

    @pl.when(jnp.logical_not(has_low))
    def _():
        for c in range(chunks):
            ext_k[c][0:RADIUS] = jnp.zeros((RADIUS,) + ext_k[c].shape[1:], jnp.bfloat16)
            ext_v[c][0:RADIUS] = jnp.zeros((RADIUS,) + ext_k[c].shape[1:], jnp.bfloat16)

    @pl.when(jnp.logical_not(has_high))
    def _():
        for c in range(chunks):
            ext_k[c][RADIUS + blocks :] = jnp.zeros((RADIUS,) + ext_k[c].shape[1:], jnp.bfloat16)
            ext_v[c][RADIUS + blocks :] = jnp.zeros((RADIUS,) + ext_k[c].shape[1:], jnp.bfloat16)

    def partial_copies(m, c):
        return (
            pltpu.make_async_remote_copy(
                src_ref=msg.at[m, :, chunk_cols(c)],
                dst_ref=got.at[m, :, chunk_cols(c)],
                send_sem=p_send.at[m, c],
                recv_sem=p_recv.at[m, c],
                device_id={"ctx": lax.rem(me + 2 * (m + 1), n)},
                device_id_type=MESH,
            ),
            pltpu.make_async_remote_copy(
                src_ref=msg_stat.at[m, c],
                dst_ref=got_stat.at[m, c],
                send_sem=ps_send.at[m, c],
                recv_sem=ps_recv.at[m, c],
                device_id={"ctx": lax.rem(me + 2 * (m + 1), n)},
                device_id_type=MESH,
            ),
        )

    for copy in kv_locals:
        copy.wait()
    for copy in locals_:
        copy.wait()

    half = lax.broadcasted_iota(jnp.int32, (1, halo + rows), 1)
    lane = lax.broadcasted_iota(jnp.int32, (own, HD), 1)

    def send_partials(c):
        first_head, count = groups[c]
        for m in range(len(others)):
            target = lax.rem(me + 2 * (m + 1), n)
            above = target > me
            start = jnp.where(above, 0, RADIUS)
            low_end = jnp.where(jnp.logical_and(above, jnp.logical_not(has_low)), halo, 0)
            high_end = jnp.where(
                jnp.logical_or(above, has_high), halo + rows, rows
            )
            valid = jnp.logical_and(half >= low_end, half < high_end)
            stats = jnp.zeros((own, HD), jnp.float32)
            for p in range(count):
                h, o = first_head + p, p * HD
                cols = slice(h * HD, (h + 1) * HD)
                span = pl.ds(start, RADIUS + blocks)
                key = ext_k[c][span, :, o : o + HD].reshape(halo + rows, HD)
                value = ext_v[c][span, :, o : o + HD].reshape(halo + rows, HD)
                scores = jnp.where(valid, dot_nt(mq_s[target, :, cols], key), LOWEST)
                peak, total, weights = softmax_parts(scores)
                msg[m, :, cols] = (dot_nn(weights, value) / total).astype(jnp.bfloat16)
                stats = jnp.where(lane == 2 * p, peak, stats)
                stats = jnp.where(lane == 2 * p + 1, total, stats)
            msg_stat[m, c] = stats.T[:8]
            for copy in partial_copies(m, c):
                copy.start()

    column = lax.broadcasted_iota(jnp.int32, (1, 2 * halo + rows + mem), 1)
    first = jnp.where(has_low, 0, halo)
    last = jnp.where(has_high, 2 * halo + rows, halo + rows)
    present = jnp.logical_or(
        jnp.logical_and(column >= first, column < last), column >= 2 * halo + rows
    )
    base = me * blocks - RADIUS

    def out_copy(c):
        cols = chunk_cols(c)
        return pltpu.make_async_copy(out_s.at[:, cols], out_h.at[:, cols], out_sem.at[c])

    def finish_memory(h):
        cols = slice(h * HD, (h + 1) * HD)
        mout_s[:, cols] = (own_sum[:, cols] / own_stat[:, heads + h : heads + h + 1]).astype(jnp.bfloat16)

    def fold_chunk(c):
        first_head, count = groups[c]
        for m in others:
            for copy in partial_copies(m, c):
                copy.wait_recv()
            columns = got_stat[m, c].T
            for p in range(count):
                h = first_head + p
                cols = slice(h * HD, (h + 1) * HD)
                peak, total = own_stat[:, h : h + 1], own_stat[:, heads + h : heads + h + 1]
                other_peak, other_total = columns[:, 2 * p : 2 * p + 1], columns[:, 2 * p + 1 : 2 * p + 2]
                joined = jnp.maximum(peak, other_peak)
                factor = jnp.exp2((peak - joined) * EXPONENT_SCALE)
                other = other_total * jnp.exp2((other_peak - joined) * EXPONENT_SCALE)
                own_sum[:, cols] = own_sum[:, cols] * factor + got[m, :, cols].astype(jnp.float32) * other
                own_stat[:, h : h + 1] = joined
                own_stat[:, heads + h : heads + h + 1] = total * factor + other
        for p in range(count):
            finish_memory(first_head + p)

    for c in range(chunks):
        @pl.when(has_low)
        def _(c=c):
            for t in range(2):
                halo_copy(c, t, True).wait_recv()

        @pl.when(has_high)
        def _(c=c):
            for t in range(2):
                halo_copy(c, t, False).wait_recv()

        send_partials(c)
        if c + AHEAD < chunks:
            send_halo(c + AHEAD)
        for p in range(groups[c][1]):
            h, o = groups[c][0] + p, p * HD
            cols = slice(h * HD, (h + 1) * HD)
            for b in range(blocks):
                near = [
                    jnp.clip(wb[b, s] - base, 0, blocks + 2 * RADIUS - 1) for s in range(wb.shape[1])
                ]
                distant = [jnp.clip(mb[b, s], 0, mem // BLK - 1) for s in range(mb.shape[1])]
                key = jnp.concatenate(
                    [ext_k[c][s, :, o : o + HD] for s in near]
                    + [mk_s[s, :, cols] for s in distant],
                    axis=0,
                )
                value = jnp.concatenate(
                    [ext_v[c][s, :, o : o + HD] for s in near]
                    + [mv_s[s, :, cols] for s in distant],
                    axis=0,
                )
                part = slice(b * BLK, (b + 1) * BLK)
                peak, total, weights = softmax_parts(dot_nt(q_s[part, cols], key))
                out_s[part, cols] = (dot_nn(weights, value) / total).astype(jnp.bfloat16)
            query = mq_s[me, :, cols]
            key = jnp.concatenate(
                [
                    ext_k[c][:, :, o : o + HD].reshape(rows + 2 * halo, HD),
                    mk_s[:, :, cols].reshape(mem, HD),
                ],
                axis=0,
            )
            value = jnp.concatenate(
                [
                    ext_v[c][:, :, o : o + HD].reshape(rows + 2 * halo, HD),
                    mv_s[:, :, cols].reshape(mem, HD),
                ],
                axis=0,
            )
            scores = jnp.where(present, dot_nt(query, key), LOWEST)
            peak, total, weights = softmax_parts(scores)
            own_sum[:, cols] = dot_nn(weights, value)
            own_stat[:, h : h + 1] = peak
            own_stat[:, heads + h : heads + h + 1] = total
        out_copy(c).start()
        if c == chunks - 1:
            for earlier in range(c):
                fold_chunk(earlier)

    fold_chunk(chunks - 1)
    mem_out = pltpu.make_async_copy(mout_s, mout_h, out_sem.at[chunks])
    mem_out.start()

    for c in range(chunks):

        @pl.when(has_high)
        def _(c=c):
            for t in range(2):
                halo_copy(c, t, True).wait_send()

        @pl.when(has_low)
        def _(c=c):
            for t in range(2):
                halo_copy(c, t, False).wait_send()

        for m in others:
            for copy in partial_copies(m, c):
                copy.wait_send()
        out_copy(c).wait()
    mem_out.wait()


def place(a_ref, m_ref, a_out, m_out, sems):
    part = a_ref.shape[0] // PIECES
    copies = [
        pltpu.make_async_copy(
            a_ref.at[pl.ds(i * part, part)], a_out.at[pl.ds(i * part, part)], sems.at[i]
        )
        for i in range(PIECES)
    ] + [pltpu.make_async_copy(m_ref, m_out, sems.at[PIECES])]
    for copy in copies:
        copy.start()
    for copy in copies:
        copy.wait()


def on_device(
    n, queries, keys, values, mem_queries, mem_keys, mem_values, window_blocks, memory_blocks
):
    rows, columns = queries.shape
    mem = mem_queries.shape[0]
    heads = columns // HD
    sizes = [2] * ((heads - 2) // 2) + [1, 1]
    groups = [(sum(sizes[:c]), size) for c, size in enumerate(sizes)]
    chunks, far = len(groups), n // 2 - 1
    own = mem // n
    ext_blocks = rows // BLK + 2 * RADIUS
    bf16, f32 = jnp.bfloat16, jnp.float32
    any_spec = pl.BlockSpec(memory_space=pl.ANY)
    smem_spec = pl.BlockSpec(memory_space=pltpu.SMEM)
    dma = pltpu.SemaphoreType.DMA
    scratch = (
        [pltpu.VMEM((ext_blocks, BLK, size * HD), bf16) for _ in range(2) for size in sizes]
        + [
            pltpu.VMEM((rows, columns), bf16),
            pltpu.VMEM((n, own, columns), bf16),
            pltpu.VMEM((mem // BLK, BLK, columns), bf16),
            pltpu.VMEM((mem // BLK, BLK, columns), bf16),
            pltpu.VMEM((rows, columns), bf16),
            pltpu.VMEM((own, columns), bf16),
            pltpu.VMEM((own, columns), f32),
            pltpu.VMEM((own, HD), f32),
            pltpu.VMEM((far, own, columns), bf16),
            pltpu.VMEM((far, chunks, 8, own), f32),
            pltpu.VMEM((far, own, columns), bf16),
            pltpu.VMEM((far, chunks, 8, own), f32),
        ]
        + [
            dma((4,)),
            dma((chunks, 2)),
            dma((chunks, 2, 2)),
            dma((chunks, 2, 2)),
            dma((far, chunks)),
            dma((far, chunks)),
            dma((far, chunks)),
            dma((far, chunks)),
            dma((chunks + 1,)),
        ]
    )

    def in_blocks(array):
        return array.reshape(-1, BLK, columns)

    attended, memory_out = pl.pallas_call(
        functools.partial(kernel, n, heads, rows, mem, groups),
        out_shape=(
            jax.ShapeDtypeStruct((rows, columns), bf16),
            jax.ShapeDtypeStruct((own, columns), bf16),
        ),
        in_specs=[smem_spec] * 2 + [any_spec] * 6,
        out_specs=(any_spec, any_spec),
        scratch_shapes=scratch,
        compiler_params=pltpu.CompilerParams(
            collective_id=0, has_side_effects=True, vmem_limit_bytes=60 << 20
        ),
        name="split_context_attention",
    )(
        window_blocks,
        memory_blocks,
        queries,
        in_blocks(keys),
        in_blocks(values),
        mem_queries.reshape(n, own, columns),
        in_blocks(mem_keys),
        in_blocks(mem_values),
    )
    return pl.pallas_call(
        place,
        out_shape=(
            jax.ShapeDtypeStruct((rows, columns), bf16),
            jax.ShapeDtypeStruct((own, columns), bf16),
        ),
        in_specs=[any_spec] * 2,
        out_specs=(any_spec, any_spec),
        scratch_shapes=[dma((PIECES + 1,))],
        compiler_params=pltpu.CompilerParams(vmem_limit_bytes=60 << 20),
        name="place",
    )(attended, memory_out)


def solution(mesh):
    in_specs = (
        P(("groups", "ctx"), ("head", "sub")),
        P(("groups", "ctx"), ("head", "sub")),
        P(("groups", "ctx"), ("head", "sub")),
        P("groups", ("head", "sub")),
        P("groups", ("head", "sub")),
        P("groups", ("head", "sub")),
        P(("groups", "ctx"), None),
        P(("groups", "ctx"), None),
    )
    out_specs = (P(("groups", "ctx"), ("head", "sub")), P(("groups", "ctx"), ("head", "sub")))
    return jax.shard_map(
        functools.partial(on_device, mesh.shape["ctx"]),
        mesh=mesh,
        in_specs=in_specs,
        out_specs=out_specs,
        check_vma=False,
    )
```

```python
import functools
import math

import jax
import jax.numpy as jnp
from jax import lax
from jax.experimental import pallas as pl
from jax.experimental.pallas import tpu as pltpu
from jax.sharding import PartitionSpec as P

HD = 128
BLK = 64
RADIUS = 4
MESH = pl.DeviceIdType.MESH
EXPONENT_SCALE = math.log2(math.e) / math.sqrt(HD)
LOWEST = -1e30
AHEAD = 8
PIECES = 4


def dot_nt(a, b):
    return lax.dot_general(a, b, (((1,), (1,)), ((), ())), preferred_element_type=jnp.float32)


def dot_nn(a, b):
    return lax.dot_general(a, b, (((1,), (0,)), ((), ())), preferred_element_type=jnp.float32)


def softmax_parts(scores):
    peak = jnp.max(scores, axis=1, keepdims=True)
    exps = jnp.exp2((scores - peak) * EXPONENT_SCALE)
    total = jnp.sum(exps, axis=1, keepdims=True)
    return peak, total, exps.astype(jnp.bfloat16)


def kernel(n, heads, rows, mem, groups, *refs):
    chunks = len(groups)
    (wb, mb, q_h, k_h, v_h, mq_h, mk_h, mv_h, out_h, mout_h) = refs[:10]
    refs = refs[10:]
    ext_k, ext_v, refs = refs[:chunks], refs[chunks : 2 * chunks], refs[2 * chunks :]
    (q_s, mq_s, mk_s, mv_s, out_s, mout_s, own_sum, own_stat, msg, msg_stat, got, got_stat) = refs[:12]
    (local_sem, kv_local, kv_send, kv_recv, p_send, p_recv, ps_send, ps_recv, out_sem) = refs[12:]

    def chunk_cols(c):
        return pl.ds(groups[c][0] * HD, groups[c][1] * HD)

    own = mem // n
    blocks = rows // BLK
    halo = RADIUS * BLK
    me = lax.axis_index("ctx")
    others = range(n // 2 - 1)
    has_low, has_high = me > 0, me < n - 1

    locals_ = [
        pltpu.make_async_copy(mq_h, mq_s, local_sem.at[0]),
        pltpu.make_async_copy(q_h, q_s, local_sem.at[1]),
        pltpu.make_async_copy(mk_h, mk_s, local_sem.at[2]),
        pltpu.make_async_copy(mv_h, mv_s, local_sem.at[3]),
    ]
    kv_locals = []
    for c in range(chunks):
        cols = chunk_cols(c)
        for t, (src, ext) in enumerate(((k_h, ext_k), (v_h, ext_v))):
            kv_locals.append(
                pltpu.make_async_copy(
                    src.at[:, :, cols], ext[c].at[pl.ds(RADIUS, blocks)], kv_local.at[c, t]
                )
            )
    locals_[0].start()
    for copy in kv_locals:
        copy.start()
    for copy in locals_[1:]:
        copy.start()

    barrier = pltpu.get_barrier_semaphore()
    for j in range(n):

        @pl.when(j != me)
        def _(j=j):
            pl.semaphore_signal(barrier, inc=1, device_id={"ctx": j}, device_id_type=MESH)

    pl.semaphore_wait(barrier, n - 1)

    high, low = jnp.minimum(me + 1, n - 1), jnp.maximum(me - 1, 0)

    def halo_copy(c, t, upward):
        src, ext = ((k_h, ext_k), (v_h, ext_v))[t]
        cols = chunk_cols(c)
        d = 0 if upward else 1
        if upward:
            part, start, target = pl.ds(blocks - RADIUS, RADIUS), 0, high
        else:
            part, start, target = pl.ds(0, RADIUS), RADIUS + blocks, low
        return pltpu.make_async_remote_copy(
            src_ref=src.at[part, :, cols],
            dst_ref=ext[c].at[pl.ds(start, RADIUS)],
            send_sem=kv_send.at[c, t, d],
            recv_sem=kv_recv.at[c, t, d],
            device_id={"ctx": target},
            device_id_type=MESH,
        )

    def send_halo(c):
        @pl.when(has_high)
        def _():
            for t in range(2):
                halo_copy(c, t, True).start()

        @pl.when(has_low)
        def _():
            for t in range(2):
                halo_copy(c, t, False).start()

    for c in range(min(AHEAD, chunks)):
        send_halo(c)

    @pl.when(jnp.logical_not(has_low))
    def _():
        for c in range(chunks):
            ext_k[c][0:RADIUS] = jnp.zeros((RADIUS,) + ext_k[c].shape[1:], jnp.bfloat16)
            ext_v[c][0:RADIUS] = jnp.zeros((RADIUS,) + ext_k[c].shape[1:], jnp.bfloat16)

    @pl.when(jnp.logical_not(has_high))
    def _():
        for c in range(chunks):
            ext_k[c][RADIUS + blocks :] = jnp.zeros((RADIUS,) + ext_k[c].shape[1:], jnp.bfloat16)
            ext_v[c][RADIUS + blocks :] = jnp.zeros((RADIUS,) + ext_k[c].shape[1:], jnp.bfloat16)

    def partial_copies(m, c):
        return (
            pltpu.make_async_remote_copy(
                src_ref=msg.at[m, :, chunk_cols(c)],
                dst_ref=got.at[m, :, chunk_cols(c)],
                send_sem=p_send.at[m, c],
                recv_sem=p_recv.at[m, c],
                device_id={"ctx": lax.rem(me + 2 * (m + 1), n)},
                device_id_type=MESH,
            ),
            pltpu.make_async_remote_copy(
                src_ref=msg_stat.at[m, c],
                dst_ref=got_stat.at[m, c],
                send_sem=ps_send.at[m, c],
                recv_sem=ps_recv.at[m, c],
                device_id={"ctx": lax.rem(me + 2 * (m + 1), n)},
                device_id_type=MESH,
            ),
        )

    for copy in kv_locals:
        copy.wait()
    for copy in locals_:
        copy.wait()

    half = lax.broadcasted_iota(jnp.int32, (1, halo + rows), 1)
    lane = lax.broadcasted_iota(jnp.int32, (own, HD), 1)

    def send_partials(c):
        first_head, count = groups[c]
        for m in range(len(others)):
            target = lax.rem(me + 2 * (m + 1), n)
            above = target > me
            start = jnp.where(above, 0, RADIUS)
            low_end = jnp.where(jnp.logical_and(above, jnp.logical_not(has_low)), halo, 0)
            high_end = jnp.where(
                jnp.logical_or(above, has_high), halo + rows, rows
            )
            valid = jnp.logical_and(half >= low_end, half < high_end)
            stats = jnp.zeros((own, HD), jnp.float32)
            for p in range(count):
                h, o = first_head + p, p * HD
                cols = slice(h * HD, (h + 1) * HD)
                span = pl.ds(start, RADIUS + blocks)
                key = ext_k[c][span, :, o : o + HD].reshape(halo + rows, HD)
                value = ext_v[c][span, :, o : o + HD].reshape(halo + rows, HD)
                scores = jnp.where(valid, dot_nt(mq_s[target, :, cols], key), LOWEST)
                peak, total, weights = softmax_parts(scores)
                msg[m, :, cols] = (dot_nn(weights, value) / total).astype(jnp.bfloat16)
                stats = jnp.where(lane == 2 * p, peak, stats)
                stats = jnp.where(lane == 2 * p + 1, total, stats)
            msg_stat[m, c] = stats.T[:8]
            for copy in partial_copies(m, c):
                copy.start()

    column = lax.broadcasted_iota(jnp.int32, (1, 2 * halo + rows + mem), 1)
    first = jnp.where(has_low, 0, halo)
    last = jnp.where(has_high, 2 * halo + rows, halo + rows)
    present = jnp.logical_or(
        jnp.logical_and(column >= first, column < last), column >= 2 * halo + rows
    )
    base = me * blocks - RADIUS

    def out_copy(c):
        cols = chunk_cols(c)
        return pltpu.make_async_copy(out_s.at[:, cols], out_h.at[:, cols], out_sem.at[c])

    def finish_memory(h):
        cols = slice(h * HD, (h + 1) * HD)
        mout_s[:, cols] = (own_sum[:, cols] / own_stat[:, heads + h : heads + h + 1]).astype(jnp.bfloat16)

    def fold_chunk(c):
        first_head, count = groups[c]
        for m in others:
            for copy in partial_copies(m, c):
                copy.wait_recv()
            columns = got_stat[m, c].T
            for p in range(count):
                h = first_head + p
                cols = slice(h * HD, (h + 1) * HD)
                peak, total = own_stat[:, h : h + 1], own_stat[:, heads + h : heads + h + 1]
                other_peak, other_total = columns[:, 2 * p : 2 * p + 1], columns[:, 2 * p + 1 : 2 * p + 2]
                joined = jnp.maximum(peak, other_peak)
                factor = jnp.exp2((peak - joined) * EXPONENT_SCALE)
                other = other_total * jnp.exp2((other_peak - joined) * EXPONENT_SCALE)
                own_sum[:, cols] = own_sum[:, cols] * factor + got[m, :, cols].astype(jnp.float32) * other
                own_stat[:, h : h + 1] = joined
                own_stat[:, heads + h : heads + h + 1] = total * factor + other
        for p in range(count):
            finish_memory(first_head + p)

    for c in range(chunks):
        @pl.when(has_low)
        def _(c=c):
            for t in range(2):
                halo_copy(c, t, True).wait_recv()

        @pl.when(has_high)
        def _(c=c):
            for t in range(2):
                halo_copy(c, t, False).wait_recv()

        send_partials(c)
        if c + AHEAD < chunks:
            send_halo(c + AHEAD)
        for p in range(groups[c][1]):
            h, o = groups[c][0] + p, p * HD
            cols = slice(h * HD, (h + 1) * HD)
            for b in range(blocks):
                near = [
                    jnp.clip(wb[b, s] - base, 0, blocks + 2 * RADIUS - 1) for s in range(wb.shape[1])
                ]
                distant = [jnp.clip(mb[b, s], 0, mem // BLK - 1) for s in range(mb.shape[1])]
                key = jnp.concatenate(
                    [ext_k[c][s, :, o : o + HD] for s in near]
                    + [mk_s[s, :, cols] for s in distant],
                    axis=0,
                )
                value = jnp.concatenate(
                    [ext_v[c][s, :, o : o + HD] for s in near]
                    + [mv_s[s, :, cols] for s in distant],
                    axis=0,
                )
                part = slice(b * BLK, (b + 1) * BLK)
                peak, total, weights = softmax_parts(dot_nt(q_s[part, cols], key))
                out_s[part, cols] = (dot_nn(weights, value) / total).astype(jnp.bfloat16)
            query = mq_s[me, :, cols]
            key = jnp.concatenate(
                [
                    ext_k[c][:, :, o : o + HD].reshape(rows + 2 * halo, HD),
                    mk_s[:, :, cols].reshape(mem, HD),
                ],
                axis=0,
            )
            value = jnp.concatenate(
                [
                    ext_v[c][:, :, o : o + HD].reshape(rows + 2 * halo, HD),
                    mv_s[:, :, cols].reshape(mem, HD),
                ],
                axis=0,
            )
            scores = jnp.where(present, dot_nt(query, key), LOWEST)
            peak, total, weights = softmax_parts(scores)
            own_sum[:, cols] = dot_nn(weights, value)
            own_stat[:, h : h + 1] = peak
            own_stat[:, heads + h : heads + h + 1] = total
        out_copy(c).start()
        if c == chunks - 1:
            for earlier in range(c):
                fold_chunk(earlier)

    fold_chunk(chunks - 1)
    mem_out = pltpu.make_async_copy(mout_s, mout_h, out_sem.at[chunks])
    mem_out.start()

    for c in range(chunks):

        @pl.when(has_high)
        def _(c=c):
            for t in range(2):
                halo_copy(c, t, True).wait_send()

        @pl.when(has_low)
        def _(c=c):
            for t in range(2):
                halo_copy(c, t, False).wait_send()

        for m in others:
            for copy in partial_copies(m, c):
                copy.wait_send()
        out_copy(c).wait()
    mem_out.wait()


def place(a_ref, m_ref, a_out, m_out, a_s, m_s, sems):
    part = a_ref.shape[0] // PIECES
    spans = [
        (ref.at[pl.ds(i * part, part)], held.at[pl.ds(i * part, part)], out.at[pl.ds(i * part, part)])
        for ref, held, out in ((a_ref, a_s, a_out),)
        for i in range(PIECES)
    ] + [(m_ref, m_s, m_out)]
    loads = [pltpu.make_async_copy(x, y, sems.at[0, i]) for i, (x, y, _) in enumerate(spans)]
    stores = [pltpu.make_async_copy(y, z, sems.at[1, i]) for i, (_, y, z) in enumerate(spans)]
    for copy in loads:
        copy.start()
    for load, store in zip(loads, stores):
        load.wait()
        store.start()
    for copy in stores:
        copy.wait()


def on_device(
    n, queries, keys, values, mem_queries, mem_keys, mem_values, window_blocks, memory_blocks
):
    rows, columns = queries.shape
    mem = mem_queries.shape[0]
    heads = columns // HD
    sizes = [2] * ((heads - 2) // 2) + [1, 1]
    groups = [(sum(sizes[:c]), size) for c, size in enumerate(sizes)]
    chunks, far = len(groups), n // 2 - 1
    own = mem // n
    ext_blocks = rows // BLK + 2 * RADIUS
    bf16, f32 = jnp.bfloat16, jnp.float32
    any_spec = pl.BlockSpec(memory_space=pl.ANY)
    smem_spec = pl.BlockSpec(memory_space=pltpu.SMEM)
    dma = pltpu.SemaphoreType.DMA
    scratch = (
        [pltpu.VMEM((ext_blocks, BLK, size * HD), bf16) for _ in range(2) for size in sizes]
        + [
            pltpu.VMEM((rows, columns), bf16),
            pltpu.VMEM((n, own, columns), bf16),
            pltpu.VMEM((mem // BLK, BLK, columns), bf16),
            pltpu.VMEM((mem // BLK, BLK, columns), bf16),
            pltpu.VMEM((rows, columns), bf16),
            pltpu.VMEM((own, columns), bf16),
            pltpu.VMEM((own, columns), f32),
            pltpu.VMEM((own, HD), f32),
            pltpu.VMEM((far, own, columns), bf16),
            pltpu.VMEM((far, chunks, 8, own), f32),
            pltpu.VMEM((far, own, columns), bf16),
            pltpu.VMEM((far, chunks, 8, own), f32),
        ]
        + [
            dma((4,)),
            dma((chunks, 2)),
            dma((chunks, 2, 2)),
            dma((chunks, 2, 2)),
            dma((far, chunks)),
            dma((far, chunks)),
            dma((far, chunks)),
            dma((far, chunks)),
            dma((chunks + 1,)),
        ]
    )

    def in_blocks(array):
        return array.reshape(-1, BLK, columns)

    attended, memory_out = pl.pallas_call(
        functools.partial(kernel, n, heads, rows, mem, groups),
        out_shape=(
            jax.ShapeDtypeStruct((rows, columns), bf16),
            jax.ShapeDtypeStruct((own, columns), bf16),
        ),
        in_specs=[smem_spec] * 2 + [any_spec] * 6,
        out_specs=(any_spec, any_spec),
        scratch_shapes=scratch,
        compiler_params=pltpu.CompilerParams(
            collective_id=0, has_side_effects=True, vmem_limit_bytes=60 << 20
        ),
        name="split_context_attention",
    )(
        window_blocks,
        memory_blocks,
        queries,
        in_blocks(keys),
        in_blocks(values),
        mem_queries.reshape(n, own, columns),
        in_blocks(mem_keys),
        in_blocks(mem_values),
    )
    return pl.pallas_call(
        place,
        out_shape=(
            jax.ShapeDtypeStruct((rows, columns), bf16),
            jax.ShapeDtypeStruct((own, columns), bf16),
        ),
        in_specs=[any_spec] * 2,
        out_specs=(any_spec, any_spec),
        scratch_shapes=[
            pltpu.VMEM((rows, columns), bf16),
            pltpu.VMEM((own, columns), bf16),
            dma((2, PIECES + 1)),
        ],
        compiler_params=pltpu.CompilerParams(vmem_limit_bytes=60 << 20),
        name="place",
    )(attended, memory_out)


def solution(mesh):
    in_specs = (
        P(("groups", "ctx"), ("head", "sub")),
        P(("groups", "ctx"), ("head", "sub")),
        P(("groups", "ctx"), ("head", "sub")),
        P("groups", ("head", "sub")),
        P("groups", ("head", "sub")),
        P("groups", ("head", "sub")),
        P(("groups", "ctx"), None),
        P(("groups", "ctx"), None),
    )
    out_specs = (P(("groups", "ctx"), ("head", "sub")), P(("groups", "ctx"), ("head", "sub")))
    return jax.shard_map(
        functools.partial(on_device, mesh.shape["ctx"]),
        mesh=mesh,
        in_specs=in_specs,
        out_specs=out_specs,
        check_vma=False,
    )
```

```python
import functools
import math

import jax
import jax.numpy as jnp
from jax import lax
from jax.experimental import pallas as pl
from jax.experimental.pallas import tpu as pltpu
from jax.sharding import PartitionSpec as P

HD = 128
BLK = 64
RADIUS = 4
MESH = pl.DeviceIdType.MESH
EXPONENT_SCALE = math.log2(math.e) / math.sqrt(HD)
LOWEST = -1e30
AHEAD = 3
PIECES = 4


def dot_nt(a, b):
    return lax.dot_general(a, b, (((1,), (1,)), ((), ())), preferred_element_type=jnp.float32)


def dot_nn(a, b):
    return lax.dot_general(a, b, (((1,), (0,)), ((), ())), preferred_element_type=jnp.float32)


def softmax_parts(scores):
    peak = jnp.max(scores, axis=1, keepdims=True)
    exps = jnp.exp2((scores - peak) * EXPONENT_SCALE)
    total = jnp.sum(exps, axis=1, keepdims=True)
    return peak, total, exps.astype(jnp.bfloat16)


def kernel(n, heads, rows, mem, groups, *refs):
    chunks = len(groups)
    (wb, mb, q_h, k_h, v_h, mq_h, mk_h, mv_h, out_h, mout_h) = refs[:10]
    refs = refs[10:]
    ext_k, ext_v, refs = refs[:chunks], refs[chunks : 2 * chunks], refs[2 * chunks :]
    (q_s, mq_s, mk_s, mv_s, out_s, mout_s, own_sum, own_stat, msg, msg_stat, got, got_stat) = refs[:12]
    (local_sem, kv_local, kv_send, kv_recv, p_send, p_recv, ps_send, ps_recv, out_sem) = refs[12:]

    def chunk_cols(c):
        return pl.ds(groups[c][0] * HD, groups[c][1] * HD)

    own = mem // n
    blocks = rows // BLK
    halo = RADIUS * BLK
    me = lax.axis_index("ctx")
    others = range(n // 2 - 1)
    has_low, has_high = me > 0, me < n - 1

    locals_ = [
        pltpu.make_async_copy(mq_h, mq_s, local_sem.at[0]),
        pltpu.make_async_copy(q_h, q_s, local_sem.at[1]),
        pltpu.make_async_copy(mk_h, mk_s, local_sem.at[2]),
        pltpu.make_async_copy(mv_h, mv_s, local_sem.at[3]),
    ]
    kv_locals = []
    for c in range(chunks):
        cols = chunk_cols(c)
        for t, (src, ext) in enumerate(((k_h, ext_k), (v_h, ext_v))):
            kv_locals.append(
                pltpu.make_async_copy(
                    src.at[:, :, cols], ext[c].at[pl.ds(RADIUS, blocks)], kv_local.at[c, t]
                )
            )
    locals_[0].start()
    for copy in kv_locals:
        copy.start()
    for copy in locals_[1:]:
        copy.start()

    barrier = pltpu.get_barrier_semaphore()
    for j in range(n):

        @pl.when(j != me)
        def _(j=j):
            pl.semaphore_signal(barrier, inc=1, device_id={"ctx": j}, device_id_type=MESH)

    pl.semaphore_wait(barrier, n - 1)

    high, low = jnp.minimum(me + 1, n - 1), jnp.maximum(me - 1, 0)

    def halo_copy(c, t, upward):
        src, ext = ((k_h, ext_k), (v_h, ext_v))[t]
        cols = chunk_cols(c)
        d = 0 if upward else 1
        if upward:
            part, start, target = pl.ds(blocks - RADIUS, RADIUS), 0, high
        else:
            part, start, target = pl.ds(0, RADIUS), RADIUS + blocks, low
        return pltpu.make_async_remote_copy(
            src_ref=src.at[part, :, cols],
            dst_ref=ext[c].at[pl.ds(start, RADIUS)],
            send_sem=kv_send.at[c, t, d],
            recv_sem=kv_recv.at[c, t, d],
            device_id={"ctx": target},
            device_id_type=MESH,
        )

    def send_halo(c):
        @pl.when(has_high)
        def _():
            for t in range(2):
                halo_copy(c, t, True).start()

        @pl.when(has_low)
        def _():
            for t in range(2):
                halo_copy(c, t, False).start()

    paced = lax.axis_index("sub") > 0
    for c in range(min(AHEAD, chunks)):
        send_halo(c)

    @pl.when(jnp.logical_not(paced))
    def _():
        for c in range(AHEAD, chunks):
            send_halo(c)

    @pl.when(jnp.logical_not(has_low))
    def _():
        for c in range(chunks):
            ext_k[c][0:RADIUS] = jnp.zeros((RADIUS,) + ext_k[c].shape[1:], jnp.bfloat16)
            ext_v[c][0:RADIUS] = jnp.zeros((RADIUS,) + ext_k[c].shape[1:], jnp.bfloat16)

    @pl.when(jnp.logical_not(has_high))
    def _():
        for c in range(chunks):
            ext_k[c][RADIUS + blocks :] = jnp.zeros((RADIUS,) + ext_k[c].shape[1:], jnp.bfloat16)
            ext_v[c][RADIUS + blocks :] = jnp.zeros((RADIUS,) + ext_k[c].shape[1:], jnp.bfloat16)

    def partial_copies(m, c):
        return (
            pltpu.make_async_remote_copy(
                src_ref=msg.at[m, :, chunk_cols(c)],
                dst_ref=got.at[m, :, chunk_cols(c)],
                send_sem=p_send.at[m, c],
                recv_sem=p_recv.at[m, c],
                device_id={"ctx": lax.rem(me + 2 * (m + 1), n)},
                device_id_type=MESH,
            ),
            pltpu.make_async_remote_copy(
                src_ref=msg_stat.at[m, c],
                dst_ref=got_stat.at[m, c],
                send_sem=ps_send.at[m, c],
                recv_sem=ps_recv.at[m, c],
                device_id={"ctx": lax.rem(me + 2 * (m + 1), n)},
                device_id_type=MESH,
            ),
        )

    for copy in kv_locals:
        copy.wait()
    for copy in locals_:
        copy.wait()

    half = lax.broadcasted_iota(jnp.int32, (1, halo + rows), 1)
    lane = lax.broadcasted_iota(jnp.int32, (own, HD), 1)

    def send_partials(c):
        first_head, count = groups[c]
        for m in range(len(others)):
            target = lax.rem(me + 2 * (m + 1), n)
            above = target > me
            start = jnp.where(above, 0, RADIUS)
            low_end = jnp.where(jnp.logical_and(above, jnp.logical_not(has_low)), halo, 0)
            high_end = jnp.where(
                jnp.logical_or(above, has_high), halo + rows, rows
            )
            valid = jnp.logical_and(half >= low_end, half < high_end)
            stats = jnp.zeros((own, HD), jnp.float32)
            for p in range(count):
                h, o = first_head + p, p * HD
                cols = slice(h * HD, (h + 1) * HD)
                span = pl.ds(start, RADIUS + blocks)
                key = ext_k[c][span, :, o : o + HD].reshape(halo + rows, HD)
                value = ext_v[c][span, :, o : o + HD].reshape(halo + rows, HD)
                scores = jnp.where(valid, dot_nt(mq_s[target, :, cols], key), LOWEST)
                peak, total, weights = softmax_parts(scores)
                msg[m, :, cols] = (dot_nn(weights, value) / total).astype(jnp.bfloat16)
                stats = jnp.where(lane == 2 * p, peak, stats)
                stats = jnp.where(lane == 2 * p + 1, total, stats)
            msg_stat[m, c] = stats.T[:8]
            for copy in partial_copies(m, c):
                copy.start()

    column = lax.broadcasted_iota(jnp.int32, (1, 2 * halo + rows + mem), 1)
    first = jnp.where(has_low, 0, halo)
    last = jnp.where(has_high, 2 * halo + rows, halo + rows)
    present = jnp.logical_or(
        jnp.logical_and(column >= first, column < last), column >= 2 * halo + rows
    )
    base = me * blocks - RADIUS

    def out_copy(c):
        cols = chunk_cols(c)
        return pltpu.make_async_copy(out_s.at[:, cols], out_h.at[:, cols], out_sem.at[c])

    def finish_memory(h):
        cols = slice(h * HD, (h + 1) * HD)
        mout_s[:, cols] = (own_sum[:, cols] / own_stat[:, heads + h : heads + h + 1]).astype(jnp.bfloat16)

    def fold_chunk(c):
        first_head, count = groups[c]
        for m in others:
            for copy in partial_copies(m, c):
                copy.wait_recv()
            columns = got_stat[m, c].T
            for p in range(count):
                h = first_head + p
                cols = slice(h * HD, (h + 1) * HD)
                peak, total = own_stat[:, h : h + 1], own_stat[:, heads + h : heads + h + 1]
                other_peak, other_total = columns[:, 2 * p : 2 * p + 1], columns[:, 2 * p + 1 : 2 * p + 2]
                joined = jnp.maximum(peak, other_peak)
                factor = jnp.exp2((peak - joined) * EXPONENT_SCALE)
                other = other_total * jnp.exp2((other_peak - joined) * EXPONENT_SCALE)
                own_sum[:, cols] = own_sum[:, cols] * factor + got[m, :, cols].astype(jnp.float32) * other
                own_stat[:, h : h + 1] = joined
                own_stat[:, heads + h : heads + h + 1] = total * factor + other
        for p in range(count):
            finish_memory(first_head + p)

    for c in range(chunks):
        @pl.when(has_low)
        def _(c=c):
            for t in range(2):
                halo_copy(c, t, True).wait_recv()

        @pl.when(has_high)
        def _(c=c):
            for t in range(2):
                halo_copy(c, t, False).wait_recv()

        send_partials(c)
        if c + AHEAD < chunks:

            @pl.when(paced)
            def _(c=c):
                send_halo(c + AHEAD)

        for p in range(groups[c][1]):
            h, o = groups[c][0] + p, p * HD
            cols = slice(h * HD, (h + 1) * HD)
            for b in range(blocks):
                near = [
                    jnp.clip(wb[b, s] - base, 0, blocks + 2 * RADIUS - 1) for s in range(wb.shape[1])
                ]
                distant = [jnp.clip(mb[b, s], 0, mem // BLK - 1) for s in range(mb.shape[1])]
                key = jnp.concatenate(
                    [ext_k[c][s, :, o : o + HD] for s in near]
                    + [mk_s[s, :, cols] for s in distant],
                    axis=0,
                )
                value = jnp.concatenate(
                    [ext_v[c][s, :, o : o + HD] for s in near]
                    + [mv_s[s, :, cols] for s in distant],
                    axis=0,
                )
                part = slice(b * BLK, (b + 1) * BLK)
                peak, total, weights = softmax_parts(dot_nt(q_s[part, cols], key))
                out_s[part, cols] = (dot_nn(weights, value) / total).astype(jnp.bfloat16)
            query = mq_s[me, :, cols]
            key = jnp.concatenate(
                [
                    ext_k[c][:, :, o : o + HD].reshape(rows + 2 * halo, HD),
                    mk_s[:, :, cols].reshape(mem, HD),
                ],
                axis=0,
            )
            value = jnp.concatenate(
                [
                    ext_v[c][:, :, o : o + HD].reshape(rows + 2 * halo, HD),
                    mv_s[:, :, cols].reshape(mem, HD),
                ],
                axis=0,
            )
            scores = jnp.where(present, dot_nt(query, key), LOWEST)
            peak, total, weights = softmax_parts(scores)
            own_sum[:, cols] = dot_nn(weights, value)
            own_stat[:, h : h + 1] = peak
            own_stat[:, heads + h : heads + h + 1] = total
        out_copy(c).start()
        if c == chunks - 1:
            for earlier in range(c):
                fold_chunk(earlier)

    fold_chunk(chunks - 1)
    mem_out = pltpu.make_async_copy(mout_s, mout_h, out_sem.at[chunks])
    mem_out.start()

    for c in range(chunks):

        @pl.when(has_high)
        def _(c=c):
            for t in range(2):
                halo_copy(c, t, True).wait_send()

        @pl.when(has_low)
        def _(c=c):
            for t in range(2):
                halo_copy(c, t, False).wait_send()

        for m in others:
            for copy in partial_copies(m, c):
                copy.wait_send()
        out_copy(c).wait()
    mem_out.wait()


def place(a_ref, m_ref, a_out, m_out, a_s, m_s, sems):
    part = a_ref.shape[0] // PIECES
    spans = [
        (ref.at[pl.ds(i * part, part)], held.at[pl.ds(i * part, part)], out.at[pl.ds(i * part, part)])
        for ref, held, out in ((a_ref, a_s, a_out),)
        for i in range(PIECES)
    ] + [(m_ref, m_s, m_out)]
    loads = [pltpu.make_async_copy(x, y, sems.at[0, i]) for i, (x, y, _) in enumerate(spans)]
    stores = [pltpu.make_async_copy(y, z, sems.at[1, i]) for i, (_, y, z) in enumerate(spans)]
    for copy in loads:
        copy.start()
    for load, store in zip(loads, stores):
        load.wait()
        store.start()
    for copy in stores:
        copy.wait()


def on_device(
    n, queries, keys, values, mem_queries, mem_keys, mem_values, window_blocks, memory_blocks
):
    rows, columns = queries.shape
    mem = mem_queries.shape[0]
    heads = columns // HD
    sizes = [2] * ((heads - 2) // 2) + [1, 1]
    groups = [(sum(sizes[:c]), size) for c, size in enumerate(sizes)]
    chunks, far = len(groups), n // 2 - 1
    own = mem // n
    ext_blocks = rows // BLK + 2 * RADIUS
    bf16, f32 = jnp.bfloat16, jnp.float32
    any_spec = pl.BlockSpec(memory_space=pl.ANY)
    smem_spec = pl.BlockSpec(memory_space=pltpu.SMEM)
    dma = pltpu.SemaphoreType.DMA
    scratch = (
        [pltpu.VMEM((ext_blocks, BLK, size * HD), bf16) for _ in range(2) for size in sizes]
        + [
            pltpu.VMEM((rows, columns), bf16),
            pltpu.VMEM((n, own, columns), bf16),
            pltpu.VMEM((mem // BLK, BLK, columns), bf16),
            pltpu.VMEM((mem // BLK, BLK, columns), bf16),
            pltpu.VMEM((rows, columns), bf16),
            pltpu.VMEM((own, columns), bf16),
            pltpu.VMEM((own, columns), f32),
            pltpu.VMEM((own, HD), f32),
            pltpu.VMEM((far, own, columns), bf16),
            pltpu.VMEM((far, chunks, 8, own), f32),
            pltpu.VMEM((far, own, columns), bf16),
            pltpu.VMEM((far, chunks, 8, own), f32),
        ]
        + [
            dma((4,)),
            dma((chunks, 2)),
            dma((chunks, 2, 2)),
            dma((chunks, 2, 2)),
            dma((far, chunks)),
            dma((far, chunks)),
            dma((far, chunks)),
            dma((far, chunks)),
            dma((chunks + 1,)),
        ]
    )

    def in_blocks(array):
        return array.reshape(-1, BLK, columns)

    attended, memory_out = pl.pallas_call(
        functools.partial(kernel, n, heads, rows, mem, groups),
        out_shape=(
            jax.ShapeDtypeStruct((rows, columns), bf16),
            jax.ShapeDtypeStruct((own, columns), bf16),
        ),
        in_specs=[smem_spec] * 2 + [any_spec] * 6,
        out_specs=(any_spec, any_spec),
        scratch_shapes=scratch,
        compiler_params=pltpu.CompilerParams(
            collective_id=0, has_side_effects=True, vmem_limit_bytes=60 << 20
        ),
        name="split_context_attention",
    )(
        window_blocks,
        memory_blocks,
        queries,
        in_blocks(keys),
        in_blocks(values),
        mem_queries.reshape(n, own, columns),
        in_blocks(mem_keys),
        in_blocks(mem_values),
    )
    return pl.pallas_call(
        place,
        out_shape=(
            jax.ShapeDtypeStruct((rows, columns), bf16),
            jax.ShapeDtypeStruct((own, columns), bf16),
        ),
        in_specs=[any_spec] * 2,
        out_specs=(any_spec, any_spec),
        scratch_shapes=[
            pltpu.VMEM((rows, columns), bf16),
            pltpu.VMEM((own, columns), bf16),
            dma((2, PIECES + 1)),
        ],
        compiler_params=pltpu.CompilerParams(vmem_limit_bytes=60 << 20),
        name="place",
    )(attended, memory_out)


def solution(mesh):
    in_specs = (
        P(("groups", "ctx"), ("head", "sub")),
        P(("groups", "ctx"), ("head", "sub")),
        P(("groups", "ctx"), ("head", "sub")),
        P("groups", ("head", "sub")),
        P("groups", ("head", "sub")),
        P("groups", ("head", "sub")),
        P(("groups", "ctx"), None),
        P(("groups", "ctx"), None),
    )
    out_specs = (P(("groups", "ctx"), ("head", "sub")), P(("groups", "ctx"), ("head", "sub")))
    return jax.shard_map(
        functools.partial(on_device, mesh.shape["ctx"]),
        mesh=mesh,
        in_specs=in_specs,
        out_specs=out_specs,
        check_vma=False,
    )
```
